32 devices in a mesh: seq: 8 (over z, y), span: 4 (over x, core).
Axes of the slice: x: 2, y: 2, z: 4, core: 2. Of those that a mesh axis runs over, the one named last changes fastest.
Arguments:
- inputs: bfloat16 [8, 512, 768], P('seq', 'span'), may hold values from -6 to 6
- norm_gain: float32 [768], replicated, may hold values from 0.1 to 1.9
- z_weight: bfloat16 [768, 1536], P(('seq', 'span')), may hold values from -0.21875 to 0.21875
- xbc_weight: bfloat16 [768, 1792], P(('seq', 'span')), may hold values from -0.21875 to 0.21875
- dt_weight: bfloat16 [768, 24], P(('seq', 'span')), may hold values from -0.21875 to 0.21875
- conv_weight: float32 [4, 1792], replicated, may hold values from -3 to 3
- conv_bias: float32 [1792], replicated, may hold values from -3 to 3
- dt_bias: float32 [24], replicated, may hold values from -6 to -1
- a_log: float32 [24], replicated, may hold values from -1 to 1.5
- skip_gain: float32 [24], replicated, may hold values from 0.5 to 1.5
- gate_gain: float32 [1536], replicated, may hold values from 0.1 to 1.9
- out_weight: bfloat16 [1536, 768], P(('seq', 'span')), may hold values from -0.15625 to 0.15625
- segments: int32 [8, 512], P('seq', 'span'), may hold values from 0 to 3, never falling along the last dimension, each value on 1 to 256 neighbouring positions
- cotangent: bfloat16 [8, 512, 768], P('seq', 'span'), may hold values from -6 to 6
Outputs:
- output: bfloat16 [8, 512, 768], P('seq', 'span')
- input_grad: float32 [8, 512, 768], P('seq', 'span')
- norm_gain_grad: float32 [768], replicated
- z_weight_grad: float32 [768, 1536], P(('seq', 'span'))
- xbc_weight_grad: float32 [768, 1792], P(('seq', 'span'))
- dt_weight_grad: float32 [768, 24], P(('seq', 'span'))
- conv_weight_grad: float32 [4, 1792], replicated
- conv_bias_grad: float32 [1792], replicated
- dt_bias_grad: float32 [24], replicated
- a_log_grad: float32 [24], replicated
- skip_gain_grad: float32 [24], replicated
- gate_gain_grad: float32 [1536], replicated
- out_weight_grad: float32 [1536, 768], P(('seq', 'span'))
The draws below stay inside these ranges and needn't reach their ends.
Inputs may be any that keep to these rules, and one draw needn't show every extreme that they name: `segments`: within a sequence the numbers never fall; a document is one run of equal numbers, of 1 to 256 tokens.
All inputs are finite; a program needn't handle non-finite values.
Results may differ from the reference program's by a relative error of at most 0.0094.
Values may be sent and summed in bfloat16 or wider, within the bound.
A program may use at most 128 MiB of HBM per device.

```python
import math
import jax
import jax.numpy as jnp
import numpy as np
from jax import lax

D = 768
DI = 1536
H = 24
P_SIZE = 64
N = 128
KW = 4
SPAN = 128
CH = 1792
LEN = 512
SEQS = 8
N_SPAN = 4


def shard_levels(own_key, shape, pieces, least, top_value):
    loudness = 1.0
    for dim, parts in pieces:
        draws = jax.random.uniform(jax.random.fold_in(jax.random.fold_in(own_key, 6), dim), (parts,), jnp.float32, least / len(pieces), top_value / len(pieces))
        loudness = loudness * jnp.repeat(jnp.exp(draws), shape[dim] // parts).reshape((-1,) + (1,) * (len(shape) - 1 - dim))
    return loudness


def split_up(amount, total, limit, slope):
    loads = [(1 << 20) // math.isqrt(standing ** slope) + 1 for standing in range(2, amount + 1)]
    rest, counts = total - limit - (amount - 1), [1] * (amount - 1)
    while rest > 0:
        movable = [i for i in range(amount - 1) if counts[i] < limit]
        pool, budget = sum([loads[i] for i in movable]), rest
        for i in movable:
            addition = min(limit - counts[i], max(1, budget * loads[i] // pool), rest)
            counts[i] = counts[i] + addition
            rest = rest - addition
    return np.array([limit] + counts)


def uneven(rng, amount, total, bound, lean):
    if amount == 2:
        one = jax.random.randint(rng, (), max(1, total - bound), min(bound, total - 1) + 1)
        return jnp.stack([one, total - one])
    tallies = jnp.asarray(split_up(amount, total, bound, lean), jnp.int32)
    twos = (amount - 1) // 2
    source_of, receiver = tallies[1:1 + 2 * twos:2], tallies[2:2 + 2 * twos:2]
    margin = jnp.minimum(source_of - 1, bound - receiver)
    moved = jax.random.randint(jax.random.fold_in(rng, 1), (twos,), 0, 1 << 20) % (margin + 1)
    tallies = tallies.at[1:1 + 2 * twos:2].set(source_of - moved).at[2:2 + 2 * twos:2].set(receiver + moved)
    return tallies[jax.random.permutation(jax.random.fold_in(rng, 2), amount)]


def centred(rng, extent, scale, reach, cuts=(), kind=jnp.bfloat16):
    entries = scale * jax.random.normal(rng, extent, jnp.float32)
    if cuts:
        entries = entries * shard_levels(rng, extent, cuts, -0.22, 0.18)
    return jnp.clip(entries, -reach, reach).astype(kind)


def setup_inputs(seed: int = 0) -> dict:
    seeds = jax.random.split(jax.random.key(seed), 15)
    return {
        "inputs": centred(seeds[0], (SEQS, LEN, D), 1.0, 6.0, ((0, 8), (1, 4))),
        "norm_gain": jnp.clip(1.0 + 0.18 * jax.random.normal(seeds[1], (D,), jnp.float32), 0.1, 1.9),
        "z_weight": centred(seeds[2], (D, DI), D ** -0.5, 0.21875, ((0, 32),)),
        "xbc_weight": centred(seeds[3], (D, CH), D ** -0.5, 0.21875, ((0, 32),)),
        "dt_weight": centred(seeds[4], (D, H), D ** -0.5, 0.21875, ((0, 32),)),
        "conv_weight": centred(seeds[5], (KW, CH), KW ** -0.5, 3.0, (), jnp.float32),
        "conv_bias": centred(seeds[6], (CH,), 0.5, 3.0, (), jnp.float32),
        "dt_bias": jnp.clip(jax.random.uniform(seeds[7], (H,), jnp.float32, -6.0, -1.0), -6.0, -1.0),
        "a_log": jnp.clip(jax.random.uniform(seeds[8], (H,), jnp.float32, -1.0, 1.5), -1.0, 1.5),
        "skip_gain": jnp.clip(jax.random.uniform(seeds[9], (H,), jnp.float32, 0.5, 1.5), 0.5, 1.5),
        "gate_gain": jnp.clip(1.0 + 0.18 * jax.random.normal(seeds[10], (DI,), jnp.float32), 0.1, 1.9),
        "out_weight": centred(seeds[11], (DI, D), DI ** -0.5, 0.15625, ((0, 32),)),
        "segments": jax.vmap(lambda own: jnp.searchsorted(jnp.cumsum(uneven(own, 4, LEN, LEN // 2, 1)), jnp.arange(LEN), side="right"))(jax.random.split(seeds[12], SEQS)).reshape((SEQS, LEN)).astype(jnp.int32),
        "cotangent": centred(seeds[13], (SEQS, LEN, D), 1.0, 6.0, ((0, 8), (1, 4))),
    }


EPSILON = 1e-05
HIGHEST = lax.Precision.HIGHEST

def input_norm(values, gain):
    scale = lax.rsqrt(lax.optimization_barrier(jnp.mean(values * values, axis=-1, keepdims=True)) + EPSILON)
    return values * scale * gain

def gated_norm(mixed, gate, gain):
    gated = mixed * jax.nn.silu(gate)
    scale = lax.rsqrt(lax.optimization_barrier(jnp.mean(gated * gated, axis=-1, keepdims=True)) + EPSILON)
    return gated * scale * gain

def conv_and_step(conv_in, edge, seg_now, seg_edge, conv_weight, conv_bias, dt_raw, dt_bias, a_log):
    taps = conv_weight.shape[0]
    length = conv_in.shape[0]
    padded = jnp.concatenate([edge, conv_in], axis=0)
    seg_all = jnp.concatenate([seg_edge, seg_now], axis=0)
    total = jnp.zeros_like(conv_in) + conv_bias
    for offset in range(taps):
        same = (seg_all[offset:offset + length] == seg_now).astype(jnp.float32)
        total = total + conv_weight[offset] * padded[offset:offset + length] * same[:, None]
    activated = jax.nn.silu(total)
    step_size = jax.nn.softplus(dt_raw + dt_bias)
    log_decay = -jnp.exp(a_log) * step_size
    return (activated, step_size, log_decay)

def scan_local(activated, step_size, log_decay, seg_now, seg_before, skip_gain):
    length = activated.shape[0]
    inner = activated[:, :DI].reshape(length, H, P_SIZE)
    in_state = activated[:, DI:DI + N]
    out_state = activated[:, DI + N:]
    cumul = jnp.cumsum(log_decay, axis=0)
    cum_heads = cumul.T
    later = lax.broadcasted_iota(jnp.int32, (length, length), 0)
    earlier = lax.broadcasted_iota(jnp.int32, (length, length), 1)
    allowed = (later >= earlier) & (seg_now[:, None] == seg_now[None, :])
    mask_three = allowed[None, :, :]
    spread = cum_heads[:, :, None] - cum_heads[:, None, :]
    decay = jnp.where(mask_three, jnp.exp(jnp.where(mask_three, spread, 0.0)), 0.0)
    intersection = jnp.dot(out_state, in_state.T, precision=HIGHEST, preferred_element_type=jnp.float32)
    mixing = intersection[None, :, :] * decay * step_size.T[:, None, :]
    result = jnp.einsum('hts,shp->thp', mixing, inner, precision=HIGHEST)
    result = result + skip_gain[None, :, None] * inner
    carried = jnp.exp(cumul) * (seg_now == seg_before).astype(jnp.float32)[:, None]
    tail = jnp.exp(cumul[-1][None, :] - cumul) * (seg_now == seg_now[-1]).astype(jnp.float32)[:, None] * step_size
    local_end = jnp.einsum('sh,shp,sn->hpn', tail, inner, in_state, precision=HIGHEST)
    return (result, local_end, carried)

def add_carry(result, carried, out_state, state_in):
    return result + carried[:, :, None] * jnp.einsum('tn,hpn->thp', out_state, state_in, precision=HIGHEST)

def span_full(conv_in, edge, dt_raw, conv_weight, conv_bias, dt_bias, a_log, skip_gain, state_in, seg_now, seg_edge):
    activated, step_size, log_decay = conv_and_step(conv_in, edge, seg_now, seg_edge, conv_weight, conv_bias, dt_raw, dt_bias, a_log)
    result, local_end, carried = scan_local(activated, step_size, log_decay, seg_now, seg_edge[-1], skip_gain)
    mixed = add_carry(result, carried, activated[:, DI + N:], state_in)
    state_end = carried[-1][:, None, None] * state_in + local_end
    return (mixed.reshape(mixed.shape[0], DI), state_end)

def by_span(values):
    return values.reshape(SEQS, N_SPAN, SPAN, values.shape[-1])

def reference(inputs, norm_gain, z_weight, xbc_weight, dt_weight, conv_weight, conv_bias, dt_bias, a_log, skip_gain, gate_gain, out_weight, segments, cotangent):
    flat = inputs.astype(jnp.float32).reshape(SEQS * LEN, D)
    normed = input_norm(flat, norm_gain).astype(jnp.bfloat16)
    gate = jnp.dot(normed, z_weight, preferred_element_type=jnp.float32)
    conv_flat = jnp.dot(normed, xbc_weight, preferred_element_type=jnp.float32).astype(jnp.bfloat16)
    dt_raw = jnp.dot(normed, dt_weight, preferred_element_type=jnp.float32)
    conv_spans = by_span(conv_flat.astype(jnp.float32))
    gate_spans = by_span(gate)
    dt_spans = by_span(dt_raw)
    seg_spans = (segments + 1).astype(jnp.float32).reshape(SEQS, N_SPAN, SPAN)
    edges = jnp.concatenate([jnp.zeros((SEQS, 1, KW - 1, CH), jnp.float32), conv_spans[:, :-1, SPAN - KW + 1:]], axis=1)
    seg_edges = jnp.concatenate([jnp.zeros((SEQS, 1, KW - 1), jnp.float32), seg_spans[:, :-1, SPAN - KW + 1:]], axis=1)
    zero_state = jnp.zeros((H, P_SIZE, N), jnp.float32)

    def states_of(conv_one, edge_one, dt_one, seg_one, sege_one):

        def forward_step(state, items):
            conv_v, edge_v, dt_v, seg_v, sege_v = items
            mixed, state_end = span_full(conv_v, edge_v, dt_v, conv_weight, conv_bias, dt_bias, a_log, skip_gain, state, seg_v, sege_v)
            return (state_end, (mixed, state))
        unused, (mixed_all, states) = lax.scan(forward_step, zero_state, (conv_one, edge_one, dt_one, seg_one, sege_one))
        return (mixed_all, states)

    def forward_one(items):
        conv_one, edge_one, gate_one, dt_one, seg_one, sege_one = items
        mixed_all, states = states_of(conv_one, edge_one, dt_one, seg_one, sege_one)
        return gated_norm(mixed_all, gate_one, gate_gain)
    normed_mix = lax.map(forward_one, (conv_spans, edges, gate_spans, dt_spans, seg_spans, seg_edges))
    mix_flat = normed_mix.reshape(SEQS * LEN, DI).astype(jnp.bfloat16)
    projected = jnp.dot(mix_flat, out_weight, preferred_element_type=jnp.float32)
    output = (flat + projected).astype(jnp.bfloat16).reshape(inputs.shape)
    grad_out = cotangent.reshape(SEQS * LEN, D)
    out_weight_grad = jnp.dot(mix_flat.T, grad_out, preferred_element_type=jnp.float32)
    grad_mix = jnp.dot(grad_out, out_weight.T, preferred_element_type=jnp.float32)
    grad_spans = by_span(grad_mix)
    small_params = (conv_weight, conv_bias, dt_bias, a_log, skip_gain, gate_gain)

    def backward_one(items):
        conv_one, edge_one, gate_one, dt_one, seg_one, sege_one, grad_one = items
        unused, states = states_of(conv_one, edge_one, dt_one, seg_one, sege_one)

        def backward_step(carry, span_items):
            state_grad, edge_next, sums = carry
            conv_v, edge_v, gate_v, dt_v, seg_v, sege_v, grad_v, state_v = span_items

            def whole(conv_a, edge_a, gate_a, dt_a, weight_a, bias_a, dtb_a, alog_a, skip_a, gain_a, state_a):
                mixed, state_end = span_full(conv_a, edge_a, dt_a, weight_a, bias_a, dtb_a, alog_a, skip_a, state_a, seg_v, sege_v)
                return (gated_norm(mixed, gate_a, gain_a), state_end)
            unused_out, pullback = jax.vjp(whole, conv_v, edge_v, gate_v, dt_v, conv_weight, conv_bias, dt_bias, a_log, skip_gain, gate_gain, state_v)
            grads = pullback((grad_v, state_grad))
            conv_grad = grads[0].at[SPAN - KW + 1:].add(edge_next)
            sums = tuple((total + part for total, part in zip(sums, grads[4:10])))
            return ((grads[10], grads[1], sums), (conv_grad, grads[2], grads[3]))
        start = (zero_state, jnp.zeros((KW - 1, CH), jnp.float32), tuple((jnp.zeros_like(param) for param in small_params)))
        (unused_grad, unused_edge, sums), (conv_g, gate_g, dt_g) = lax.scan(backward_step, start, (conv_one, edge_one, gate_one, dt_one, seg_one, sege_one, grad_one, states), reverse=True)
        return (conv_g, gate_g, dt_g, sums)
    conv_g, gate_g, dt_g, sums = lax.map(backward_one, (conv_spans, edges, gate_spans, dt_spans, seg_spans, seg_edges, grad_spans))
    small_grads = tuple((lax.optimization_barrier(jnp.sum(part, axis=0)) for part in sums))
    gate_b = gate_g.reshape(SEQS * LEN, DI).astype(jnp.bfloat16)
    conv_b = conv_g.reshape(SEQS * LEN, CH).astype(jnp.bfloat16)
    dt_b = dt_g.reshape(SEQS * LEN, H).astype(jnp.bfloat16)
    z_weight_grad = jnp.dot(normed.T, gate_b, preferred_element_type=jnp.float32)
    xbc_weight_grad = jnp.dot(normed.T, conv_b, preferred_element_type=jnp.float32)
    dt_weight_grad = jnp.dot(normed.T, dt_b, preferred_element_type=jnp.float32)
    normed_grad = jnp.dot(gate_b, z_weight.T, preferred_element_type=jnp.float32)
    normed_grad = normed_grad + jnp.dot(conv_b, xbc_weight.T, preferred_element_type=jnp.float32)
    normed_grad = normed_grad + jnp.dot(dt_b, dt_weight.T, preferred_element_type=jnp.float32)
    unused_norm, norm_pull = jax.vjp(input_norm, flat, norm_gain)
    grad_flat, norm_gain_grad = norm_pull(normed_grad)
    input_grad = (grad_out.astype(jnp.float32) + grad_flat).reshape(inputs.shape)
    return (output, input_grad, norm_gain_grad, z_weight_grad, xbc_weight_grad, dt_weight_grad, small_grads[0], small_grads[1], small_grads[2], small_grads[3], small_grads[4], small_grads[5], out_weight_grad)
```

```python
import jax
import jax.numpy as jnp
from jax import lax
from jax.experimental import pallas as pl
from jax.experimental.pallas import tpu as pltpu
from jax.sharding import PartitionSpec as P

DI = 1536
H = 24
P_SIZE = 64
N = 128
KW = 4
CH = 1792


MESH = pl.DeviceIdType.MESH
AXES = ("seq", "span")
VMEM_ROOM = 56 << 20


def bit_orders(devices, span):
    total = devices.bit_length() - 1
    inner = span.bit_length() - 1
    first = list(range(1, inner))
    outer = list(range(inner, total))
    low, high = outer[: max(1, len(outer) // 3)], outer[max(1, len(outer) // 3) :]
    return (
        [0] + first + low + high,
        [0] + low + first + high,
        [0] + high[:1] + first + low + high[1:],
    )


def device_of(me, span, bits):
    number = flipped(me, bits)
    return (number // span, number % span)


def flipped(me, bits):
    number = me
    for b in bits:
        number = number + (1 - 2 * ((me // (1 << b)) % 2)) * (1 << b)
    return number


def mask_bits(rel, order):
    levels = len(order)
    return [order[k] for k in range(levels) if (rel >> (levels - 1 - k)) & 1]


def entry(me, span, levels):
    barrier = pltpu.get_barrier_semaphore()
    for b in range(levels):
        pl.semaphore_signal(
            barrier, inc=1, device_id=device_of(me, span, [b]), device_id_type=MESH
        )
    pl.semaphore_wait(barrier, levels)


def gather_kernel(orders, span, *refs):
    streams = len(orders)
    ins, outs = refs[:streams], refs[streams : 2 * streams]
    send_sem, recv_sem, own_sem = refs[2 * streams :]
    levels = len(orders[0])
    me = lax.axis_index("seq") * span + lax.axis_index("span")
    own = []
    for c in range(streams):
        copy = pltpu.make_async_copy(ins[c], outs[c].at[me], own_sem.at[c])
        copy.start()
        own.append(copy)
    entry(me, span, levels)

    def send(c, j, m):
        order = orders[c]
        base = 1 << (levels - 1 - m) if m < levels else 0
        for r in range(base, max(1, 2 * base)):
            shard = flipped(me, mask_bits(r, order))
            pltpu.make_async_remote_copy(
                src_ref=ins[c] if m == levels else outs[c].at[shard],
                dst_ref=outs[c].at[shard],
                send_sem=send_sem.at[c, j, m],
                recv_sem=recv_sem.at[c, j, m],
                device_id=device_of(me, span, [order[j]]),
                device_id_type=MESH,
            ).start()

    def await_piece(sem, c, j, m):
        size = 1 << (levels - 1 - m) if m < levels else 1
        part = outs[c].at[pl.ds(0, size)]
        pltpu.make_async_copy(part, part, sem.at[c, j, m]).wait()

    for j in reversed(range(levels)):
        for c in range(streams):
            send(c, j, levels)
    for m in reversed(range(levels)):
        for c in range(streams):
            for p in range(levels, m, -1):
                await_piece(recv_sem, c, m, p)
            for j in reversed(range(m)):
                send(c, j, m)
    for c in range(streams):
        own[c].wait()
        for j in range(levels):
            for m in range(j + 1, levels + 1):
                await_piece(send_sem, c, j, m)


def gather_rows(arrays, mesh_shape):
    seq, span = mesh_shape
    devices = seq * span
    orders = bit_orders(devices, span)[: len(arrays)]
    levels = len(orders[0])
    sems = pltpu.SemaphoreType.DMA((len(arrays), levels, levels + 1))
    return pl.pallas_call(
        lambda *refs: gather_kernel(orders, span, *refs),
        out_shape=[jax.ShapeDtypeStruct((devices,) + a.shape, a.dtype) for a in arrays],
        in_specs=[pl.BlockSpec(memory_space=pl.ANY)] * len(arrays),
        out_specs=[pl.BlockSpec(memory_space=pl.ANY)] * len(arrays),
        scratch_shapes=[sems, sems, pltpu.SemaphoreType.DMA((len(arrays),))],
        compiler_params=pltpu.CompilerParams(collective_id=0, has_side_effects=True),
    )(*arrays)


def fold(x):
    half = x.shape[1] // 2
    return jnp.concatenate([x[:, :half], x[:, half:]], axis=0)


def unfold(x):
    half = x.shape[0] // 2
    return jnp.concatenate([x[:half], x[half:]], axis=1)


def scatter_kernel(orders, span, *refs):
    streams = len(orders)
    parts, small = refs[:streams], refs[streams]
    outs, small_out = refs[streams + 1 : 2 * streams + 1], refs[2 * streams + 1]
    rest = refs[2 * streams + 2 :]
    sent, got = rest[:streams], rest[streams : 2 * streams]
    small_sent, small_got, send_sem, recv_sem, small_send, small_recv = rest[2 * streams :]
    levels = len(orders[0])
    me = lax.axis_index("seq") * span + lax.axis_index("span")
    entry(me, span, levels)

    def total(c, j, rel):
        order = orders[c]
        shard = jnp.int32(0)
        for k, b in enumerate(order):
            mine = (me // (1 << b)) % 2
            other = (rel // (1 << (levels - 1 - k))) % 2
            shard = shard + (mine + other - 2 * mine * other) * (1 << b)
        value = parts[c][shard]
        folded = value.shape[0] != got[c].shape[1]
        value = fold(value) if folded else value
        for i in range(j):
            value = value + got[c][(1 << (levels - 1 - i)) + rel].astype(jnp.float32)
        return value, folded

    def piece(c, j, m):
        head = 1 << (levels - 1 - j)
        base = 1 << (levels - 1 - m) if m < levels else 0
        size = max(1, base)
        place = pl.ds(head + base, size)
        return size, head + base, pltpu.make_async_remote_copy(
            src_ref=sent[c].at[place],
            dst_ref=got[c].at[place],
            send_sem=send_sem.at[c, j, m],
            recv_sem=recv_sem.at[c, j, m],
            device_id=device_of(me, span, [orders[c][j]]),
            device_id_type=MESH,
        )

    def small_copy(j):
        return pltpu.make_async_remote_copy(
            src_ref=small_sent.at[j],
            dst_ref=small_got.at[j],
            send_sem=small_send.at[j],
            recv_sem=small_recv.at[j],
            device_id=device_of(me, span, [orders[0][j]]),
            device_id_type=MESH,
        )

    running = small[...]
    for j in range(levels):
        if j:
            small_copy(j - 1).wait_recv()
            running = running + small_got[j - 1]
        small_sent[j] = running
        small_copy(j).start()
        for m in range(j + 1, levels + 1):
            for c in range(streams):
                if m == j + 1:
                    for i in range(j):
                        piece(c, i, j)[2].wait_recv()
                size, start, copy = piece(c, j, m)

                def one(r, carry):
                    sent[c][start + r] = total(c, j, start + r)[0].astype(jnp.bfloat16)
                    return carry

                lax.fori_loop(0, size, one, 0)
                copy.start()
    for c in range(streams):
        for i in range(levels):
            piece(c, i, levels)[2].wait_recv()
        value, folded = total(c, levels, 0)
        outs[c][...] = unfold(value) if folded else value
    small_copy(levels - 1).wait_recv()
    small_out[...] = running + small_got[levels - 1]
    for j in range(levels):
        small_copy(j).wait_send()
        for c in range(streams):
            for m in range(j + 1, levels + 1):
                piece(c, j, m)[2].wait_send()


def wire_shape(shape):
    rows, columns = shape
    return (rows, columns) if rows % 16 == 0 else (2 * rows, columns // 2)


def scatter_room(parts):
    return sum((4 * p.size + 2 * 2 * p.size) for p in parts)


def scatter_sums(parts, small, mesh_shape):
    seq, span = mesh_shape
    devices = seq * span
    orders = bit_orders(devices, span)[: len(parts)]
    levels = len(orders[0])
    wires = [pltpu.VMEM((devices,) + wire_shape(p.shape[1:]), jnp.bfloat16) for p in parts]
    sems = pltpu.SemaphoreType.DMA((len(parts), levels, levels + 1))
    smalls = pltpu.VMEM((levels,) + small.shape, jnp.float32)
    vmem = pl.BlockSpec(memory_space=pltpu.VMEM)
    return pl.pallas_call(
        lambda *refs: scatter_kernel(orders, span, *refs),
        out_shape=[jax.ShapeDtypeStruct(p.shape[1:], jnp.float32) for p in parts]
        + [jax.ShapeDtypeStruct(small.shape, jnp.float32)],
        in_specs=[vmem] * (len(parts) + 1),
        out_specs=[vmem] * (len(parts) + 1),
        scratch_shapes=wires
        + wires
        + [
            smalls,
            smalls,
            sems,
            sems,
            pltpu.SemaphoreType.DMA((levels,)),
            pltpu.SemaphoreType.DMA((levels,)),
        ],
        compiler_params=pltpu.CompilerParams(collective_id=1, has_side_effects=True),
    )(*parts, small)


def pad_columns(x, to):
    return jnp.pad(x, ((0, 0), (0, to - x.shape[1])))


def up_to(n, multiple):
    return -(-n // multiple) * multiple


EPSILON = 1e-05
HIGHEST = lax.Precision.HIGHEST
CONTRACT_LAST = (((1,), (1,)), ((), ()))
CONTRACT_FIRST = (((0,), (0,)), ((), ()))


def shifted(x, axis, by):
    devices = lax.axis_size(axis)
    pairs = [(i, i + by) for i in range(devices) if 0 <= i + by < devices]
    return lax.ppermute(x, axis, pairs)


def carried_in(decay, state, axis, reverse):
    count = lax.axis_size(axis)
    way = -1 if reverse else 1
    heads, n = decay.shape[-1], state.shape[-1]
    row = jnp.zeros((state.shape[0], 1) + state.shape[2:], jnp.float32)
    row = row.at[:, 0, 0, :heads].set(decay)
    payload = jnp.concatenate([state, row], axis=1).astype(jnp.bfloat16)
    total = jnp.zeros_like(state)
    factor = jnp.ones_like(decay)
    for far in range(1, count):
        there = shifted(payload, axis, way * far).astype(jnp.float32)
        total = total + factor[:, :, None, None] * there[:, :heads]
        factor = factor * there[:, heads, 0, :heads]
    return total


def input_norm(values, gain):
    scale = lax.rsqrt(jnp.mean(values * values, axis=-1, keepdims=True) + EPSILON)
    return values * scale * gain


def gated_norm(mixed, gate, gain):
    gated = mixed * jax.nn.silu(gate)
    scale = lax.rsqrt(jnp.mean(gated * gated, axis=-1, keepdims=True) + EPSILON)
    return gated * scale * gain


def conv_and_step(conv_in, edge, seg_now, seg_edge, conv_weight, conv_bias, dt_raw, dt_bias, a_log):
    taps = conv_weight.shape[0]
    length = conv_in.shape[0]
    padded = jnp.concatenate([edge, conv_in], axis=0)
    seg_all = jnp.concatenate([seg_edge, seg_now], axis=0)
    total = jnp.zeros_like(conv_in) + conv_bias
    for offset in range(taps):
        same = (seg_all[offset : offset + length] == seg_now).astype(jnp.float32)
        total = total + conv_weight[offset] * padded[offset : offset + length] * same[:, None]
    activated = jax.nn.silu(total)
    step_size = jax.nn.softplus(dt_raw + dt_bias)
    log_decay = -jnp.exp(a_log) * step_size
    return (activated, step_size, log_decay)


def scan_local(activated, step_size, log_decay, seg_now, seg_before, skip_gain):
    length = activated.shape[0]
    inner = activated[:, :DI].reshape(length, H, P_SIZE)
    in_state = activated[:, DI : DI + N]
    out_state = activated[:, DI + N :]
    cumul = jnp.cumsum(log_decay, axis=0)
    cum_heads = cumul.T
    later = lax.broadcasted_iota(jnp.int32, (length, length), 0)
    earlier = lax.broadcasted_iota(jnp.int32, (length, length), 1)
    allowed = (later >= earlier) & (seg_now[:, None] == seg_now[None, :])
    mask_three = allowed[None, :, :]
    spread = cum_heads[:, :, None] - cum_heads[:, None, :]
    decay = jnp.where(mask_three, jnp.exp(jnp.where(mask_three, spread, 0.0)), 0.0)
    intersection = jnp.dot(
        out_state, in_state.T, precision=HIGHEST, preferred_element_type=jnp.float32
    )
    mixing = intersection[None, :, :] * decay * step_size.T[:, None, :]
    result = jnp.einsum("hts,shp->thp", mixing, inner, precision=HIGHEST)
    result = result + skip_gain[None, :, None] * inner
    carried = jnp.exp(cumul) * (seg_now == seg_before).astype(jnp.float32)[:, None]
    tail = (
        jnp.exp(cumul[-1][None, :] - cumul)
        * (seg_now == seg_now[-1]).astype(jnp.float32)[:, None]
        * step_size
    )
    local_end = jnp.einsum("sh,shp,sn->hpn", tail, inner, in_state, precision=HIGHEST)
    return (result, local_end, carried)


def add_carry(result, carried, out_state, state_in):
    return result + carried[:, :, None] * jnp.einsum(
        "tn,hpn->thp", out_state, state_in, precision=HIGHEST
    )


def span_full(
    conv_in,
    edge,
    dt_raw,
    conv_weight,
    conv_bias,
    dt_bias,
    a_log,
    skip_gain,
    state_in,
    seg_now,
    seg_edge,
):
    activated, step_size, log_decay = conv_and_step(
        conv_in, edge, seg_now, seg_edge, conv_weight, conv_bias, dt_raw, dt_bias, a_log
    )
    result, local_end, carried = scan_local(
        activated, step_size, log_decay, seg_now, seg_edge[-1], skip_gain
    )
    mixed = add_carry(result, carried, activated[:, DI + N :], state_in)
    state_end = carried[-1][:, None, None] * state_in + local_end
    return (mixed.reshape(mixed.shape[0], DI), state_end)


def body(
    inputs,
    norm_gain,
    z_weight,
    xbc_weight,
    dt_weight,
    conv_weight,
    conv_bias,
    dt_bias,
    a_log,
    skip_gain,
    gate_gain,
    out_weight,
    segments,
    cotangent,
):
    seqs_here, span_len, width = inputs.shape
    rows = seqs_here * span_len
    flat = inputs.astype(jnp.float32).reshape(rows, width)
    normed = input_norm(flat, norm_gain).astype(jnp.bfloat16)
    mesh_shape = (lax.axis_size("seq"), lax.axis_size("span"))
    dt_wide = up_to(H, 128)
    zdt_all, xbc_all, out_all = gather_rows(
        (
            jnp.concatenate([z_weight, pad_columns(dt_weight, dt_wide)], axis=1),
            xbc_weight,
            out_weight,
        ),
        mesh_shape,
    )
    zdt_all = zdt_all.reshape(-1, DI + dt_wide)
    xbc_all = xbc_all.reshape(-1, CH)
    out_all = out_all.reshape(-1, width)
    gate_dt = jnp.dot(normed, zdt_all, preferred_element_type=jnp.float32)
    gate, dt_raw = gate_dt[:, :DI], gate_dt[:, DI : DI + H]
    conv_wide = jnp.dot(normed, xbc_all, preferred_element_type=jnp.float32)
    conv_in = conv_wide.astype(jnp.bfloat16).reshape(seqs_here, span_len, CH)
    seg_wire = (segments[:, span_len - KW + 1 :] + 1).astype(jnp.bfloat16)
    edge, seg_edge = shifted((conv_in[:, span_len - KW + 1 :], seg_wire), "span", 1)
    conv_float = conv_in.astype(jnp.float32)
    edge_float = edge.astype(jnp.float32)
    seg_edge_float = seg_edge.astype(jnp.float32)
    seg_now = (segments + 1).astype(jnp.float32)
    dt_spans = dt_raw.reshape(seqs_here, span_len, H)
    prepare = jax.vmap(conv_and_step, in_axes=(0, 0, 0, 0, None, None, 0, None, None))
    activated, step_size, log_decay = prepare(
        conv_float,
        edge_float,
        seg_now,
        seg_edge_float,
        conv_weight,
        conv_bias,
        dt_spans,
        dt_bias,
        a_log,
    )
    local_scan = jax.vmap(scan_local, in_axes=(0, 0, 0, 0, 0, None))
    result, local_end, carried = local_scan(
        activated, step_size, log_decay, seg_now, seg_edge_float[:, -1], skip_gain
    )
    decay_total = carried[:, -1]
    state_in = carried_in(decay_total, local_end, "span", False)
    out_state = activated[:, :, DI + N :]
    mixed = jax.vmap(add_carry)(result, carried, out_state, state_in).reshape(rows, DI)
    mix_bf = gated_norm(mixed, gate, gate_gain).astype(jnp.bfloat16)
    columns = mix_bf
    projected = jnp.dot(
        columns,
        out_all,
        preferred_element_type=jnp.float32,
    )
    output = (flat + projected).astype(jnp.bfloat16).reshape(inputs.shape)
    grad_out = cotangent.reshape(rows, width)
    grad_mix = lax.dot_general(
        grad_out,
        out_all,
        CONTRACT_LAST,
        preferred_element_type=jnp.float32,
    )
    unused_norm, gate_pull = jax.vjp(gated_norm, mixed, gate, gate_gain)
    grad_mixed, grad_gate, gate_gain_grad = gate_pull(grad_mix)
    grad_heads = grad_mixed.reshape(seqs_here, span_len, H, P_SIZE)
    summary = jnp.einsum("sth,sthp,stn->shpn", carried, grad_heads, out_state, precision=HIGHEST)
    state_grad = carried_in(decay_total, summary, "span", True)

    def local_span(conv_a, edge_a, dt_a, weight_a, bias_a, dtb_a, alog_a, skip_a, state_a):
        batched = jax.vmap(span_full, in_axes=(0, 0, 0, None, None, None, None, None, 0, 0, 0))
        return batched(
            conv_a,
            edge_a,
            dt_a,
            weight_a,
            bias_a,
            dtb_a,
            alog_a,
            skip_a,
            state_a,
            seg_now,
            seg_edge_float,
        )

    unused_span, span_pull = jax.vjp(
        local_span,
        conv_float,
        edge_float,
        dt_spans,
        conv_weight,
        conv_bias,
        dt_bias,
        a_log,
        skip_gain,
        state_in,
    )
    grads = span_pull((grad_mixed.reshape(seqs_here, span_len, DI), state_grad))
    edge_back = shifted(grads[1], "span", -1)
    conv_grad = grads[0].at[:, span_len - KW + 1 :].add(edge_back)
    gate_bf = grad_gate.astype(jnp.bfloat16)
    conv_bf = conv_grad.reshape(rows, CH).astype(jnp.bfloat16)
    dt_bf = grads[2].reshape(rows, H).astype(jnp.bfloat16)
    dt_padded = pad_columns(dt_bf, dt_wide)
    normed_grad = lax.dot_general(
        jnp.concatenate([gate_bf, dt_padded], axis=1),
        zdt_all,
        CONTRACT_LAST,
        preferred_element_type=jnp.float32,
    ) + lax.dot_general(conv_bf, xbc_all, CONTRACT_LAST, preferred_element_type=jnp.float32)
    unused_input, norm_pull = jax.vjp(input_norm, flat, norm_gain)
    grad_flat, norm_gain_part = norm_pull(normed_grad)
    input_grad = (grad_out.astype(jnp.float32) + grad_flat).reshape(inputs.shape)
    smalls = (norm_gain_part, grads[3], grads[4], grads[5], grads[6], grads[7], gate_gain_grad)
    zdt_grad = jnp.concatenate([gate_bf, pad_columns(dt_bf, 2 * dt_wide)], axis=1)
    partials = tuple(
        lax.dot_general(left, right, CONTRACT_FIRST, preferred_element_type=jnp.float32)
        for left, right in ((normed, zdt_grad), (normed, conv_bf), (mix_bf, grad_out))
    )
    devices = mesh_shape[0] * mesh_shape[1]
    if scatter_room(partials) < VMEM_ROOM and all(p.shape[0] // devices % 8 == 0 for p in partials):
        flat_small = jnp.concatenate([a.reshape(-1) for a in smalls])
        padded = jnp.pad(flat_small, (0, up_to(flat_small.size, 1024) - flat_small.size))
        zdt_own, xbc_weight_grad, out_weight_grad, small_sum = scatter_sums(
            tuple(p.reshape(devices, -1, p.shape[1]) for p in partials),
            padded.reshape(-1, 128),
            mesh_shape,
        )
        small_sum = small_sum.reshape(-1)
        summed, begin = [], 0
        for a in smalls:
            summed.append(small_sum[begin : begin + a.size].reshape(a.shape))
            begin += a.size
    else:
        zdt_own, xbc_weight_grad, out_weight_grad = tuple(
            lax.psum_scatter(p, AXES, scatter_dimension=0, tiled=True) for p in partials
        )
        summed = lax.psum(smalls, AXES)
    return (
        output,
        input_grad,
        summed[0],
        zdt_own[:, :DI],
        xbc_weight_grad,
        zdt_own[:, DI : DI + H],
        summed[1],
        summed[2],
        summed[3],
        summed[4],
        summed[5],
        summed[6],
        out_weight_grad,
    )


def solution(mesh):
    in_specs = (
        P("seq", "span", None),
        P(),
        P(("seq", "span"), None),
        P(("seq", "span"), None),
        P(("seq", "span"), None),
        P(),
        P(),
        P(),
        P(),
        P(),
        P(),
        P(("seq", "span"), None),
        P("seq", "span"),
        P("seq", "span", None),
    )
    out_specs = (
        P("seq", "span", None),
        P("seq", "span", None),
        P(),
        P(("seq", "span"), None),
        P(("seq", "span"), None),
        P(("seq", "span"), None),
        P(),
        P(),
        P(),
        P(),
        P(),
        P(),
        P(("seq", "span"), None),
    )
    return jax.shard_map(body, mesh=mesh, in_specs=in_specs, out_specs=out_specs, check_vma=False)
```

```python
import jax
import jax.numpy as jnp
from jax import lax
from jax.experimental import pallas as pl
from jax.experimental.pallas import tpu as pltpu
from jax.sharding import PartitionSpec as P

DI = 1536
H = 24
P_SIZE = 64
N = 128
KW = 4
CH = 1792


MESH = pl.DeviceIdType.MESH
AXES = ("seq", "span")
VMEM_ROOM = 56 << 20


def bit_orders(devices, span):
    total = devices.bit_length() - 1
    inner = span.bit_length() - 1
    first = list(range(1, inner))
    outer = list(range(inner, total))
    low, high = outer[: max(1, len(outer) // 3)], outer[max(1, len(outer) // 3) :]
    return (
        [0] + first + low + high,
        [0] + low + first + high,
        [0] + high[:1] + first + low + high[1:],
    )


def device_of(me, span, bits):
    number = flipped(me, bits)
    return (number // span, number % span)


def flipped(me, bits):
    number = me
    for b in bits:
        number = number + (1 - 2 * ((me // (1 << b)) % 2)) * (1 << b)
    return number


def mask_bits(rel, order):
    levels = len(order)
    return [order[k] for k in range(levels) if (rel >> (levels - 1 - k)) & 1]


def entry(me, span, levels):
    barrier = pltpu.get_barrier_semaphore()
    for b in range(levels):
        pl.semaphore_signal(
            barrier, inc=1, device_id=device_of(me, span, [b]), device_id_type=MESH
        )
    pl.semaphore_wait(barrier, levels)


def gather_kernel(orders, span, *refs):
    streams = len(orders)
    ins, outs = refs[:streams], refs[streams : 2 * streams]
    send_sem, recv_sem, own_sem = refs[2 * streams :]
    levels = len(orders[0])
    me = lax.axis_index("seq") * span + lax.axis_index("span")
    own = []
    for c in range(streams):
        copy = pltpu.make_async_copy(ins[c], outs[c].at[me], own_sem.at[c])
        copy.start()
        own.append(copy)
    entry(me, span, levels)

    def send(c, j, m):
        order = orders[c]
        base = 1 << (levels - 1 - m) if m < levels else 0
        for r in range(base, max(1, 2 * base)):
            shard = flipped(me, mask_bits(r, order))
            pltpu.make_async_remote_copy(
                src_ref=ins[c] if m == levels else outs[c].at[shard],
                dst_ref=outs[c].at[shard],
                send_sem=send_sem.at[c, j, m],
                recv_sem=recv_sem.at[c, j, m],
                device_id=device_of(me, span, [order[j]]),
                device_id_type=MESH,
            ).start()

    def await_piece(sem, c, j, m):
        size = 1 << (levels - 1 - m) if m < levels else 1
        part = outs[c].at[pl.ds(0, size)]
        pltpu.make_async_copy(part, part, sem.at[c, j, m]).wait()

    for j in reversed(range(levels)):
        for c in range(streams):
            send(c, j, levels)
    for m in reversed(range(levels)):
        for c in range(streams):
            for p in range(levels, m, -1):
                await_piece(recv_sem, c, m, p)
            for j in reversed(range(m)):
                send(c, j, m)
    for c in range(streams):
        own[c].wait()
        for j in range(levels):
            for m in range(j + 1, levels + 1):
                await_piece(send_sem, c, j, m)


def gather_rows(arrays, mesh_shape):
    seq, span = mesh_shape
    devices = seq * span
    orders = bit_orders(devices, span)[: len(arrays)]
    levels = len(orders[0])
    sems = pltpu.SemaphoreType.DMA((len(arrays), levels, levels + 1))
    return pl.pallas_call(
        lambda *refs: gather_kernel(orders, span, *refs),
        out_shape=[jax.ShapeDtypeStruct((devices,) + a.shape, a.dtype) for a in arrays],
        in_specs=[pl.BlockSpec(memory_space=pl.ANY)] * len(arrays),
        out_specs=[pl.BlockSpec(memory_space=pl.ANY)] * len(arrays),
        scratch_shapes=[sems, sems, pltpu.SemaphoreType.DMA((len(arrays),))],
        compiler_params=pltpu.CompilerParams(collective_id=0, has_side_effects=True),
    )(*arrays)


def fold(x):
    half = x.shape[1] // 2
    return jnp.concatenate([x[:, :half], x[:, half:]], axis=0)


def unfold(x):
    half = x.shape[0] // 2
    return jnp.concatenate([x[:half], x[half:]], axis=1)


def small_places(shapes, width):
    places, row, column = [], 0, 0
    for rows, columns in shapes:
        if column and (rows > 1 or column + columns > width):
            row, column = row + 1, 0
        places.append((row, column))
        column += up_to(columns, 128)
        if rows > 1 or column >= width:
            row, column = row + rows, 0
    return places, up_to(row + (column > 0), 8)


def scatter_kernel(orders, span, places, widths, *refs):
    streams, smalls = len(orders), len(places)
    lefts, rights = refs[:streams], refs[streams : 2 * streams]
    refs = refs[2 * streams :]
    small_in, refs = refs[:smalls], refs[smalls:]
    outs, refs = refs[: sum(map(len, widths))], refs[sum(map(len, widths)) :]
    small_out, rest = refs[:smalls], refs[smalls:]
    parts, rest = rest[:streams], rest[streams:]
    sent, got = rest[:streams], rest[streams : 2 * streams]
    small_sent, small_got, send_sem, recv_sem, small_send, small_recv = rest[2 * streams :]
    levels = len(orders[0])
    me = lax.axis_index("seq") * span + lax.axis_index("span")
    entry(me, span, levels)

    def total(c, j, rel):
        order = orders[c]
        shard = jnp.int32(0)
        for k, b in enumerate(order):
            mine = (me // (1 << b)) % 2
            other = (rel // (1 << (levels - 1 - k))) % 2
            shard = shard + (mine + other - 2 * mine * other) * (1 << b)
        value = parts[c][shard]
        folded = value.shape[0] != got[c].shape[1]
        value = fold(value) if folded else value
        for i in range(j):
            value = value + got[c][(1 << (levels - 1 - i)) + rel].astype(jnp.float32)
        return value, folded

    def piece(c, j, m):
        head = 1 << (levels - 1 - j)
        base = 1 << (levels - 1 - m) if m < levels else 0
        size = max(1, base)
        place = pl.ds(head + base, size)
        return size, head + base, pltpu.make_async_remote_copy(
            src_ref=sent[c].at[place],
            dst_ref=got[c].at[place],
            send_sem=send_sem.at[c, j, m],
            recv_sem=recv_sem.at[c, j, m],
            device_id=device_of(me, span, [orders[c][j]]),
            device_id_type=MESH,
        )

    def small_copy(j):
        return pltpu.make_async_remote_copy(
            src_ref=small_sent.at[j],
            dst_ref=small_got.at[j],
            send_sem=small_send.at[j],
            recv_sem=small_recv.at[j],
            device_id=device_of(me, span, [orders[0][j]]),
            device_id_type=MESH,
        )

    def multiply(c):
        devices, rows, columns = parts[c].shape
        block = devices // 2
        for half in range(2):
            left = lefts[c][:, half * block * rows : (half + 1) * block * rows]
            product = lax.dot_general(
                left, rights[c][...], CONTRACT_FIRST, preferred_element_type=jnp.float32
            )
            parts[c][half * block : (half + 1) * block] = product.reshape(block, rows, columns)

    small_sent[0] = jnp.zeros(small_sent.shape[1:], jnp.float32)
    for ref, (row, column) in zip(small_in, places):
        rows, columns = ref.shape
        small_sent[0, row : row + rows, column : column + columns] = ref[...]
    running = small_sent[0]
    for j in range(levels):
        if j:
            small_copy(j - 1).wait_recv()
            running = running + small_got[j - 1]
            small_sent[j] = running
        small_copy(j).start()
        for m in range(j + 1, levels + 1):
            for c in range(streams):
                if m == 1:
                    multiply(c)
                if m == j + 1:
                    for i in range(j):
                        piece(c, i, j)[2].wait_recv()
                size, start, copy = piece(c, j, m)

                def one(r, carry):
                    sent[c][start + r] = total(c, j, start + r)[0].astype(jnp.bfloat16)
                    return carry

                lax.fori_loop(0, size, one, 0)
                copy.start()
    slot = 0
    for c in range(streams):
        for i in range(levels):
            piece(c, i, levels)[2].wait_recv()
        value, folded = total(c, levels, 0)
        value = unfold(value) if folded else value
        for begin, columns in widths[c]:
            outs[slot][...] = value[:, begin : begin + columns]
            slot += 1
    small_copy(levels - 1).wait_recv()
    small_got[levels - 1] = running + small_got[levels - 1]
    for ref, (row, column) in zip(small_out, places):
        rows, columns = ref.shape
        ref[...] = small_got[levels - 1, row : row + rows, column : column + columns]
    for j in range(levels):
        small_copy(j).wait_send()
        for c in range(streams):
            for m in range(j + 1, levels + 1):
                piece(c, j, m)[2].wait_send()


def wire_shape(shape):
    rows, columns = shape
    return (rows, columns) if rows % 16 == 0 else (2 * rows, columns // 2)


def scatter_room(pairs):
    return sum(8 * left.shape[1] * right.shape[1] for left, right in pairs)


def scatter_sums(pairs, widths, smalls, mesh_shape):
    seq, span = mesh_shape
    devices = seq * span
    orders = bit_orders(devices, span)[: len(pairs)]
    levels = len(orders[0])
    shapes = [(left.shape[1] // devices, right.shape[1]) for left, right in pairs]
    small_width = up_to(max(a.shape[1] for a in smalls), 128)
    places, small_rows = small_places([a.shape for a in smalls], small_width)
    parts = [pltpu.VMEM((devices,) + shape, jnp.float32) for shape in shapes]
    wires = [pltpu.VMEM((devices,) + wire_shape(shape), jnp.bfloat16) for shape in shapes]
    sems = pltpu.SemaphoreType.DMA((len(pairs), levels, levels + 1))
    small_wire = pltpu.VMEM((levels, small_rows, small_width), jnp.float32)
    vmem = pl.BlockSpec(memory_space=pltpu.VMEM)
    owned = [
        jax.ShapeDtypeStruct((shape[0], columns), jnp.float32)
        for shape, cuts in zip(shapes, widths)
        for begin, columns in cuts
    ]
    return pl.pallas_call(
        lambda *refs: scatter_kernel(orders, span, places, widths, *refs),
        out_shape=owned + [jax.ShapeDtypeStruct(a.shape, jnp.float32) for a in smalls],
        in_specs=[vmem] * (2 * len(pairs) + len(smalls)),
        out_specs=[vmem] * (len(owned) + len(smalls)),
        scratch_shapes=parts
        + wires
        + wires
        + [
            small_wire,
            small_wire,
            sems,
            sems,
            pltpu.SemaphoreType.DMA((levels,)),
            pltpu.SemaphoreType.DMA((levels,)),
        ],
        compiler_params=pltpu.CompilerParams(collective_id=1, has_side_effects=True),
    )(*[left for left, right in pairs], *[right for left, right in pairs], *smalls)


def pad_columns(x, to):
    return jnp.pad(x, ((0, 0), (0, to - x.shape[1])))


def up_to(n, multiple):
    return -(-n // multiple) * multiple


EPSILON = 1e-05
HIGHEST = lax.Precision.HIGH
CONTRACT_LAST = (((1,), (1,)), ((), ()))
CONTRACT_FIRST = (((0,), (0,)), ((), ()))


def shifted(x, axis, by):
    devices = lax.axis_size(axis)
    pairs = [(i, i + by) for i in range(devices) if 0 <= i + by < devices]
    return lax.ppermute(x, axis, pairs)


def carried_in(decay, state, axis, reverse):
    count = lax.axis_size(axis)
    way = -1 if reverse else 1
    heads, n = decay.shape[-1], state.shape[-1]
    row = jnp.zeros((state.shape[0], 1) + state.shape[2:], jnp.float32)
    row = row.at[:, 0, 0, :heads].set(decay)
    payload = jnp.concatenate([state, row], axis=1).astype(jnp.bfloat16)
    total = jnp.zeros_like(state)
    factor = jnp.ones_like(decay)
    for far in range(1, count):
        there = shifted(payload, axis, way * far)
        total = total + factor[:, :, None, None] * there[:, :heads].astype(jnp.float32)
        if far < count - 1:
            factor = factor * there[:, heads, 0, :heads].astype(jnp.float32)
    return total


def input_norm(values, gain):
    scale = lax.rsqrt(jnp.mean(values * values, axis=-1, keepdims=True) + EPSILON)
    return values * scale * gain


def gated_norm(mixed, gate, gain):
    gated = mixed * jax.nn.silu(gate)
    scale = lax.rsqrt(jnp.mean(gated * gated, axis=-1, keepdims=True) + EPSILON)
    return gated * scale * gain


def conv_and_step(conv_in, edge, seg_now, seg_edge, conv_weight, conv_bias, dt_raw, dt_bias, a_log):
    taps = conv_weight.shape[0]
    length = conv_in.shape[0]
    padded = jnp.concatenate([edge, conv_in], axis=0)
    seg_all = jnp.concatenate([seg_edge, seg_now], axis=0)
    total = jnp.zeros_like(conv_in) + conv_bias
    for offset in range(taps):
        same = (seg_all[offset : offset + length] == seg_now).astype(jnp.float32)
        total = total + conv_weight[offset] * padded[offset : offset + length] * same[:, None]
    activated = jax.nn.silu(total)
    step_size = jax.nn.softplus(dt_raw + dt_bias)
    log_decay = -jnp.exp(a_log) * step_size
    return (activated, step_size, log_decay)


def scan_local(activated, step_size, log_decay, seg_now, seg_before, skip_gain):
    length = activated.shape[0]
    inner = activated[:, :DI].reshape(length, H, P_SIZE)
    in_state = activated[:, DI : DI + N]
    out_state = activated[:, DI + N :]
    cumul = jnp.cumsum(log_decay, axis=0)
    cum_heads = cumul.T
    later = lax.broadcasted_iota(jnp.int32, (length, length), 0)
    earlier = lax.broadcasted_iota(jnp.int32, (length, length), 1)
    allowed = (later >= earlier) & (seg_now[:, None] == seg_now[None, :])
    mask_three = allowed[None, :, :]
    spread = cum_heads[:, :, None] - cum_heads[:, None, :]
    decay = jnp.where(mask_three, jnp.exp(jnp.where(mask_three, spread, 0.0)), 0.0)
    intersection = jnp.dot(
        out_state, in_state.T, precision=HIGHEST, preferred_element_type=jnp.float32
    )
    mixing = intersection[None, :, :] * decay * step_size.T[:, None, :]
    result = jnp.einsum("hts,shp->thp", mixing, inner, precision=HIGHEST)
    result = result + skip_gain[None, :, None] * inner
    carried = jnp.exp(cumul) * (seg_now == seg_before).astype(jnp.float32)[:, None]
    tail = (
        jnp.exp(cumul[-1][None, :] - cumul)
        * (seg_now == seg_now[-1]).astype(jnp.float32)[:, None]
        * step_size
    )
    local_end = jnp.einsum("sh,shp,sn->hpn", tail, inner, in_state, precision=HIGHEST)
    return (result, local_end, carried)


def add_carry(result, carried, out_state, state_in):
    return result + carried[:, :, None] * jnp.einsum(
        "tn,hpn->thp", out_state, state_in, precision=HIGHEST
    )


def span_full(
    conv_in,
    edge,
    dt_raw,
    conv_weight,
    conv_bias,
    dt_bias,
    a_log,
    skip_gain,
    state_in,
    seg_now,
    seg_edge,
):
    activated, step_size, log_decay = conv_and_step(
        conv_in, edge, seg_now, seg_edge, conv_weight, conv_bias, dt_raw, dt_bias, a_log
    )
    result, local_end, carried = scan_local(
        activated, step_size, log_decay, seg_now, seg_edge[-1], skip_gain
    )
    mixed = add_carry(result, carried, activated[:, DI + N :], state_in)
    state_end = carried[-1][:, None, None] * state_in + local_end
    return (mixed.reshape(mixed.shape[0], DI), state_end)


def body(
    inputs,
    norm_gain,
    z_weight,
    xbc_weight,
    dt_weight,
    conv_weight,
    conv_bias,
    dt_bias,
    a_log,
    skip_gain,
    gate_gain,
    out_weight,
    segments,
    cotangent,
):
    seqs_here, span_len, width = inputs.shape
    rows = seqs_here * span_len
    flat = inputs.astype(jnp.float32).reshape(rows, width)
    normed = input_norm(flat, norm_gain).astype(jnp.bfloat16)
    mesh_shape = (lax.axis_size("seq"), lax.axis_size("span"))
    dt_wide = up_to(H, 128)
    zdt_all, xbc_all, out_all = gather_rows(
        (
            jnp.concatenate([z_weight, pad_columns(dt_weight, dt_wide)], axis=1),
            xbc_weight,
            out_weight,
        ),
        mesh_shape,
    )
    zdt_all = zdt_all.reshape(-1, DI + dt_wide)
    xbc_all = xbc_all.reshape(-1, CH)
    out_all = out_all.reshape(-1, width)
    gate_dt = jnp.dot(normed, zdt_all, preferred_element_type=jnp.float32)
    gate, dt_raw = gate_dt[:, :DI], gate_dt[:, DI : DI + H]
    conv_wide = jnp.dot(normed, xbc_all, preferred_element_type=jnp.float32)
    conv_in = conv_wide.astype(jnp.bfloat16).reshape(seqs_here, span_len, CH)
    seg_wire = (segments[:, span_len - KW + 1 :] + 1).astype(jnp.bfloat16)
    edge, seg_edge = shifted((conv_in[:, span_len - KW + 1 :], seg_wire), "span", 1)
    conv_float = conv_in.astype(jnp.float32)
    edge_float = edge.astype(jnp.float32)
    seg_edge_float = seg_edge.astype(jnp.float32)
    seg_now = (segments + 1).astype(jnp.float32)
    dt_spans = dt_raw.reshape(seqs_here, span_len, H)
    prepare = jax.vmap(conv_and_step, in_axes=(0, 0, 0, 0, None, None, 0, None, None))
    activated, step_size, log_decay = prepare(
        conv_float,
        edge_float,
        seg_now,
        seg_edge_float,
        conv_weight,
        conv_bias,
        dt_spans,
        dt_bias,
        a_log,
    )
    local_scan = jax.vmap(scan_local, in_axes=(0, 0, 0, 0, 0, None))
    result, local_end, carried = local_scan(
        activated, step_size, log_decay, seg_now, seg_edge_float[:, -1], skip_gain
    )
    decay_total = carried[:, -1]
    state_in = carried_in(decay_total, local_end, "span", False)
    out_state = activated[:, :, DI + N :]
    mixed = jax.vmap(add_carry)(result, carried, out_state, state_in).reshape(rows, DI)
    mix_bf = gated_norm(mixed, gate, gate_gain).astype(jnp.bfloat16)
    columns = mix_bf
    projected = jnp.dot(
        columns,
        out_all,
        preferred_element_type=jnp.float32,
    )
    output = (flat + projected).astype(jnp.bfloat16).reshape(inputs.shape)
    grad_out = cotangent.reshape(rows, width)
    grad_mix = lax.dot_general(
        grad_out,
        out_all,
        CONTRACT_LAST,
        preferred_element_type=jnp.float32,
    )
    unused_norm, gate_pull = jax.vjp(gated_norm, mixed, gate, gate_gain)
    grad_mixed, grad_gate, gate_gain_grad = gate_pull(grad_mix)
    grad_heads = grad_mixed.reshape(seqs_here, span_len, H, P_SIZE)
    summary = jnp.einsum("sth,sthp,stn->shpn", carried, grad_heads, out_state, precision=HIGHEST)
    state_grad = carried_in(decay_total, summary, "span", True)

    def local_span(conv_a, edge_a, dt_a, weight_a, bias_a, dtb_a, alog_a, skip_a, state_a):
        batched = jax.vmap(span_full, in_axes=(0, 0, 0, None, None, None, None, None, 0, 0, 0))
        return batched(
            conv_a,
            edge_a,
            dt_a,
            weight_a,
            bias_a,
            dtb_a,
            alog_a,
            skip_a,
            state_a,
            seg_now,
            seg_edge_float,
        )

    unused_span, span_pull = jax.vjp(
        local_span,
        conv_float,
        edge_float,
        dt_spans,
        conv_weight,
        conv_bias,
        dt_bias,
        a_log,
        skip_gain,
        state_in,
    )
    grads = span_pull((grad_mixed.reshape(seqs_here, span_len, DI), state_grad))
    edge_back = shifted(grads[1], "span", -1)
    conv_grad = grads[0].at[:, span_len - KW + 1 :].add(edge_back)
    gate_bf = grad_gate.astype(jnp.bfloat16)
    conv_bf = conv_grad.reshape(rows, CH).astype(jnp.bfloat16)
    dt_bf = grads[2].reshape(rows, H).astype(jnp.bfloat16)
    dt_padded = pad_columns(dt_bf, dt_wide)
    normed_grad = lax.dot_general(
        jnp.concatenate([gate_bf, dt_padded], axis=1),
        zdt_all,
        CONTRACT_LAST,
        preferred_element_type=jnp.float32,
    ) + lax.dot_general(conv_bf, xbc_all, CONTRACT_LAST, preferred_element_type=jnp.float32)
    unused_input, norm_pull = jax.vjp(input_norm, flat, norm_gain)
    grad_flat, norm_gain_part = norm_pull(normed_grad)
    input_grad = (grad_out.astype(jnp.float32) + grad_flat).reshape(inputs.shape)
    smalls = (norm_gain_part, grads[3], grads[4], grads[5], grads[6], grads[7], gate_gain_grad)
    zdt_grad = jnp.concatenate([gate_bf, pad_columns(dt_bf, 2 * dt_wide)], axis=1)
    pairs = ((normed, zdt_grad), (normed, conv_bf), (mix_bf, grad_out))
    widths = (((0, DI), (DI, H)), ((0, CH),), ((0, width),))
    devices = mesh_shape[0] * mesh_shape[1]
    if scatter_room(pairs) < VMEM_ROOM and all(
        left.shape[1] // devices % 8 == 0 and left.shape[1] % 256 == 0 for left, right in pairs
    ):
        results = scatter_sums(
            pairs, widths, [a.reshape(-1, a.shape[-1]) for a in smalls], mesh_shape
        )
        z_weight_grad, dt_weight_grad, xbc_weight_grad, out_weight_grad = results[:4]
        summed = [r.reshape(a.shape) for r, a in zip(results[4:], smalls)]
    else:
        zdt_own, xbc_weight_grad, out_weight_grad = tuple(
            lax.psum_scatter(
                lax.dot_general(left, right, CONTRACT_FIRST, preferred_element_type=jnp.float32),
                AXES,
                scatter_dimension=0,
                tiled=True,
            )
            for left, right in pairs
        )
        z_weight_grad, dt_weight_grad = zdt_own[:, :DI], zdt_own[:, DI : DI + H]
        summed = lax.psum(smalls, AXES)
    return (
        output,
        input_grad,
        summed[0],
        z_weight_grad,
        xbc_weight_grad,
        dt_weight_grad,
        summed[1],
        summed[2],
        summed[3],
        summed[4],
        summed[5],
        summed[6],
        out_weight_grad,
    )


def solution(mesh):
    in_specs = (
        P("seq", "span", None),
        P(),
        P(("seq", "span"), None),
        P(("seq", "span"), None),
        P(("seq", "span"), None),
        P(),
        P(),
        P(),
        P(),
        P(),
        P(),
        P(("seq", "span"), None),
        P("seq", "span"),
        P("seq", "span", None),
    )
    out_specs = (
        P("seq", "span", None),
        P("seq", "span", None),
        P(),
        P(("seq", "span"), None),
        P(("seq", "span"), None),
        P(("seq", "span"), None),
        P(),
        P(),
        P(),
        P(),
        P(),
        P(),
        P(("seq", "span"), None),
    )
    return jax.shard_map(body, mesh=mesh, in_specs=in_specs, out_specs=out_specs, check_vma=False)
```

```python
import jax
import jax.numpy as jnp
from jax import lax
from jax.experimental import pallas as pl
from jax.experimental.pallas import tpu as pltpu
from jax.sharding import PartitionSpec as P

DI = 1536
H = 24
P_SIZE = 64
N = 128
KW = 4
CH = 1792


MESH = pl.DeviceIdType.MESH
AXES = ("seq", "span")
VMEM_ROOM = 56 << 20


def bit_orders(devices, span):
    total = devices.bit_length() - 1
    inner = span.bit_length() - 1
    first = list(range(1, inner))
    outer = list(range(inner, total))
    low, high = outer[: max(1, len(outer) // 3)], outer[max(1, len(outer) // 3) :]
    return (
        [0] + first + low + high,
        [0] + low + first + high,
        [0] + high[:1] + first + low + high[1:],
    )


def device_of(me, span, bits):
    number = flipped(me, bits)
    return (number // span, number % span)


def flipped(me, bits):
    number = me
    for b in bits:
        number = number + (1 - 2 * ((me // (1 << b)) % 2)) * (1 << b)
    return number


def mask_bits(rel, order):
    levels = len(order)
    return [order[k] for k in range(levels) if (rel >> (levels - 1 - k)) & 1]


def entry(me, span, levels):
    barrier = pltpu.get_barrier_semaphore()
    for b in range(levels):
        pl.semaphore_signal(
            barrier, inc=1, device_id=device_of(me, span, [b]), device_id_type=MESH
        )
    pl.semaphore_wait(barrier, levels)


def gather_kernel(orders, span, *refs):
    streams = len(orders)
    ins, outs = refs[:streams], refs[streams : 2 * streams]
    send_sem, recv_sem, own_sem = refs[2 * streams :]
    levels = len(orders[0])
    me = lax.axis_index("seq") * span + lax.axis_index("span")
    own = []
    for c in range(streams):
        copy = pltpu.make_async_copy(ins[c], outs[c].at[me], own_sem.at[c])
        copy.start()
        own.append(copy)
    entry(me, span, levels)

    def send(c, j, m):
        order = orders[c]
        base = 1 << (levels - 1 - m) if m < levels else 0
        for r in range(base, max(1, 2 * base)):
            shard = flipped(me, mask_bits(r, order))
            pltpu.make_async_remote_copy(
                src_ref=ins[c] if m == levels else outs[c].at[shard],
                dst_ref=outs[c].at[shard],
                send_sem=send_sem.at[c, j, m],
                recv_sem=recv_sem.at[c, j, m],
                device_id=device_of(me, span, [order[j]]),
                device_id_type=MESH,
            ).start()

    def await_piece(sem, c, j, m):
        size = 1 << (levels - 1 - m) if m < levels else 1
        part = outs[c].at[pl.ds(0, size)]
        pltpu.make_async_copy(part, part, sem.at[c, j, m]).wait()

    for j in reversed(range(levels)):
        for c in range(streams):
            send(c, j, levels)
    for m in reversed(range(levels)):
        for c in range(streams):
            for p in range(levels, m, -1):
                await_piece(recv_sem, c, m, p)
            for j in reversed(range(m)):
                send(c, j, m)
    for c in range(streams):
        own[c].wait()
        for j in range(levels):
            for m in range(j + 1, levels + 1):
                await_piece(send_sem, c, j, m)


def gather_rows(arrays, mesh_shape):
    seq, span = mesh_shape
    devices = seq * span
    orders = bit_orders(devices, span)[: len(arrays)]
    levels = len(orders[0])
    sems = pltpu.SemaphoreType.DMA((len(arrays), levels, levels + 1))
    return pl.pallas_call(
        lambda *refs: gather_kernel(orders, span, *refs),
        out_shape=[jax.ShapeDtypeStruct((devices,) + a.shape, a.dtype) for a in arrays],
        in_specs=[pl.BlockSpec(memory_space=pl.ANY)] * len(arrays),
        out_specs=[pl.BlockSpec(memory_space=pl.ANY)] * len(arrays),
        scratch_shapes=[sems, sems, pltpu.SemaphoreType.DMA((len(arrays),))],
        compiler_params=pltpu.CompilerParams(collective_id=0, has_side_effects=True),
    )(*arrays)


def fold(x):
    half = x.shape[1] // 2
    return jnp.concatenate([x[:, :half], x[:, half:]], axis=0)


def unfold(x):
    half = x.shape[0] // 2
    return jnp.concatenate([x[:half], x[half:]], axis=1)


def small_places(shapes, width):
    places, row, column = [], 0, 0
    for rows, columns in shapes:
        if column and (rows > 1 or column + columns > width):
            row, column = row + 1, 0
        places.append((row, column))
        column += up_to(columns, 128)
        if rows > 1 or column >= width:
            row, column = row + rows, 0
    return places, up_to(row + (column > 0), 8)


def scatter_kernel(orders, span, places, widths, *refs):
    streams, smalls = len(orders), len(places)
    lefts, rights = refs[:streams], refs[streams : 2 * streams]
    refs = refs[2 * streams :]
    small_in, refs = refs[:smalls], refs[smalls:]
    outs, refs = refs[: sum(map(len, widths))], refs[sum(map(len, widths)) :]
    small_out, rest = refs[:smalls], refs[smalls:]
    parts, rest = rest[:streams], rest[streams:]
    sent, got = rest[:streams], rest[streams : 2 * streams]
    small_sent, small_got, send_sem, recv_sem, small_send, small_recv = rest[2 * streams :]
    levels = len(orders[0])
    me = lax.axis_index("seq") * span + lax.axis_index("span")
    entry(me, span, levels)

    def total(c, j, rel):
        order = orders[c]
        shard = jnp.int32(0)
        for k, b in enumerate(order):
            mine = (me // (1 << b)) % 2
            other = (rel // (1 << (levels - 1 - k))) % 2
            shard = shard + (mine + other - 2 * mine * other) * (1 << b)
        value = parts[c][shard]
        folded = value.shape[0] != got[c].shape[1]
        value = fold(value) if folded else value
        for i in range(j):
            value = value + got[c][(1 << (levels - 1 - i)) + rel].astype(jnp.float32)
        return value, folded

    def piece(c, j, m):
        head = 1 << (levels - 1 - j)
        base = 1 << (levels - 1 - m) if m < levels else 0
        size = max(1, base)
        place = pl.ds(head + base, size)
        return size, head + base, pltpu.make_async_remote_copy(
            src_ref=sent[c].at[place],
            dst_ref=got[c].at[place],
            send_sem=send_sem.at[c, j, m],
            recv_sem=recv_sem.at[c, j, m],
            device_id=device_of(me, span, [orders[c][j]]),
            device_id_type=MESH,
        )

    def small_copy(j):
        return pltpu.make_async_remote_copy(
            src_ref=small_sent.at[j],
            dst_ref=small_got.at[j],
            send_sem=small_send.at[j],
            recv_sem=small_recv.at[j],
            device_id=device_of(me, span, [orders[0][j]]),
            device_id_type=MESH,
        )

    def multiply(c):
        devices, rows, columns = parts[c].shape
        block = devices // 2
        for half in range(2):
            left = lefts[c][:, half * block * rows : (half + 1) * block * rows]
            product = lax.dot_general(
                left, rights[c][...], CONTRACT_FIRST, preferred_element_type=jnp.float32
            )
            parts[c][half * block : (half + 1) * block] = product.reshape(block, rows, columns)

    small_sent[0] = jnp.zeros(small_sent.shape[1:], jnp.float32)
    for ref, (row, column) in zip(small_in, places):
        rows, columns = ref.shape
        small_sent[0, row : row + rows, column : column + columns] = ref[...]
    running = small_sent[0]
    for j in range(levels):
        if j:
            small_copy(j - 1).wait_recv()
            running = running + small_got[j - 1]
            small_sent[j] = running
        small_copy(j).start()
        for m in range(j + 1, levels + 1):
            for c in range(streams):
                if m == 1:
                    multiply(c)
                if m == j + 1:
                    for i in range(j):
                        piece(c, i, j)[2].wait_recv()
                size, start, copy = piece(c, j, m)

                def one(r, carry):
                    sent[c][start + r] = total(c, j, start + r)[0].astype(jnp.bfloat16)
                    return carry

                lax.fori_loop(0, size, one, 0)
                copy.start()
    slot = 0
    for c in range(streams):
        for i in range(levels):
            piece(c, i, levels)[2].wait_recv()
        value, folded = total(c, levels, 0)
        value = unfold(value) if folded else value
        for begin, columns in widths[c]:
            outs[slot][...] = value[:, begin : begin + columns]
            slot += 1
    small_copy(levels - 1).wait_recv()
    small_got[levels - 1] = running + small_got[levels - 1]
    for ref, (row, column) in zip(small_out, places):
        rows, columns = ref.shape
        ref[...] = small_got[levels - 1, row : row + rows, column : column + columns]
    for j in range(levels):
        small_copy(j).wait_send()
        for c in range(streams):
            for m in range(j + 1, levels + 1):
                piece(c, j, m)[2].wait_send()


def wire_shape(shape):
    rows, columns = shape
    return (rows, columns) if rows % 16 == 0 else (2 * rows, columns // 2)


def scatter_room(pairs):
    return sum(8 * left.shape[1] * right.shape[1] for left, right in pairs)


def scatter_sums(pairs, widths, smalls, mesh_shape):
    seq, span = mesh_shape
    devices = seq * span
    orders = bit_orders(devices, span)[: len(pairs)]
    levels = len(orders[0])
    shapes = [(left.shape[1] // devices, right.shape[1]) for left, right in pairs]
    small_width = up_to(max(a.shape[1] for a in smalls), 128)
    places, small_rows = small_places([a.shape for a in smalls], small_width)
    parts = [pltpu.VMEM((devices,) + shape, jnp.float32) for shape in shapes]
    wires = [pltpu.VMEM((devices,) + wire_shape(shape), jnp.bfloat16) for shape in shapes]
    sems = pltpu.SemaphoreType.DMA((len(pairs), levels, levels + 1))
    small_wire = pltpu.VMEM((levels, small_rows, small_width), jnp.float32)
    vmem = pl.BlockSpec(memory_space=pltpu.VMEM)
    owned = [
        jax.ShapeDtypeStruct((shape[0], columns), jnp.float32)
        for shape, cuts in zip(shapes, widths)
        for begin, columns in cuts
    ]
    return pl.pallas_call(
        lambda *refs: scatter_kernel(orders, span, places, widths, *refs),
        out_shape=owned + [jax.ShapeDtypeStruct(a.shape, jnp.float32) for a in smalls],
        in_specs=[vmem] * (2 * len(pairs) + len(smalls)),
        out_specs=[vmem] * (len(owned) + len(smalls)),
        scratch_shapes=parts
        + wires
        + wires
        + [
            small_wire,
            small_wire,
            sems,
            sems,
            pltpu.SemaphoreType.DMA((levels,)),
            pltpu.SemaphoreType.DMA((levels,)),
        ],
        compiler_params=pltpu.CompilerParams(collective_id=1, has_side_effects=True),
    )(*[left for left, right in pairs], *[right for left, right in pairs], *smalls)


def pad_columns(x, to):
    return jnp.pad(x, ((0, 0), (0, to - x.shape[1])))


def up_to(n, multiple):
    return -(-n // multiple) * multiple


EPSILON = 1e-05
HIGHEST = lax.Precision.DEFAULT
CONTRACT_LAST = (((1,), (1,)), ((), ()))
CONTRACT_FIRST = (((0,), (0,)), ((), ()))


def shifted(x, axis, by):
    devices = lax.axis_size(axis)
    pairs = [(i, i + by) for i in range(devices) if 0 <= i + by < devices]
    return lax.ppermute(x, axis, pairs)


def carried_in(decay, state, axis, reverse):
    count = lax.axis_size(axis)
    way = -1 if reverse else 1
    heads, n = decay.shape[-1], state.shape[-1]
    row = jnp.zeros((state.shape[0], 1) + state.shape[2:], jnp.float32)
    row = row.at[:, 0, 0, :heads].set(decay)
    payload = jnp.concatenate([state, row], axis=1).astype(jnp.bfloat16)
    total = jnp.zeros_like(state)
    factor = jnp.ones_like(decay)
    for far in range(1, count):
        there = shifted(payload, axis, way * far)
        total = total + factor[:, :, None, None] * there[:, :heads].astype(jnp.float32)
        if far < count - 1:
            factor = factor * there[:, heads, 0, :heads].astype(jnp.float32)
    return total


def input_norm(values, gain):
    scale = lax.rsqrt(jnp.mean(values * values, axis=-1, keepdims=True) + EPSILON)
    return values * scale * gain


def gated_norm(mixed, gate, gain):
    gated = mixed * jax.nn.silu(gate)
    scale = lax.rsqrt(jnp.mean(gated * gated, axis=-1, keepdims=True) + EPSILON)
    return gated * scale * gain


def conv_and_step(conv_in, edge, seg_now, seg_edge, conv_weight, conv_bias, dt_raw, dt_bias, a_log):
    taps = conv_weight.shape[0]
    length = conv_in.shape[0]
    padded = jnp.concatenate([edge, conv_in], axis=0)
    seg_all = jnp.concatenate([seg_edge, seg_now], axis=0)
    total = jnp.zeros_like(conv_in) + conv_bias
    for offset in range(taps):
        same = (seg_all[offset : offset + length] == seg_now).astype(jnp.float32)
        total = total + conv_weight[offset] * padded[offset : offset + length] * same[:, None]
    activated = jax.nn.silu(total)
    step_size = jax.nn.softplus(dt_raw + dt_bias)
    log_decay = -jnp.exp(a_log) * step_size
    return (activated, step_size, log_decay)


def scan_local(activated, step_size, log_decay, seg_now, seg_before, skip_gain):
    length = activated.shape[0]
    inner = activated[:, :DI].reshape(length, H, P_SIZE)
    in_state = activated[:, DI : DI + N]
    out_state = activated[:, DI + N :]
    cumul = jnp.cumsum(log_decay, axis=0)
    cum_heads = cumul.T
    later = lax.broadcasted_iota(jnp.int32, (length, length), 0)
    earlier = lax.broadcasted_iota(jnp.int32, (length, length), 1)
    allowed = (later >= earlier) & (seg_now[:, None] == seg_now[None, :])
    mask_three = allowed[None, :, :]
    spread = cum_heads[:, :, None] - cum_heads[:, None, :]
    decay = jnp.where(mask_three, jnp.exp(jnp.where(mask_three, spread, 0.0)), 0.0)
    intersection = jnp.dot(
        out_state, in_state.T, precision=HIGHEST, preferred_element_type=jnp.float32
    )
    mixing = intersection[None, :, :] * decay * step_size.T[:, None, :]
    result = jnp.einsum("hts,shp->thp", mixing, inner, precision=HIGHEST)
    result = result + skip_gain[None, :, None] * inner
    carried = jnp.exp(cumul) * (seg_now == seg_before).astype(jnp.float32)[:, None]
    tail = (
        jnp.exp(cumul[-1][None, :] - cumul)
        * (seg_now == seg_now[-1]).astype(jnp.float32)[:, None]
        * step_size
    )
    local_end = jnp.einsum("sh,shp,sn->hpn", tail, inner, in_state, precision=HIGHEST)
    return (result, local_end, carried)


def add_carry(result, carried, out_state, state_in):
    return result + carried[:, :, None] * jnp.einsum(
        "tn,hpn->thp", out_state, state_in, precision=HIGHEST
    )


def span_full(
    conv_in,
    edge,
    dt_raw,
    conv_weight,
    conv_bias,
    dt_bias,
    a_log,
    skip_gain,
    state_in,
    seg_now,
    seg_edge,
):
    activated, step_size, log_decay = conv_and_step(
        conv_in, edge, seg_now, seg_edge, conv_weight, conv_bias, dt_raw, dt_bias, a_log
    )
    result, local_end, carried = scan_local(
        activated, step_size, log_decay, seg_now, seg_edge[-1], skip_gain
    )
    mixed = add_carry(result, carried, activated[:, DI + N :], state_in)
    state_end = carried[-1][:, None, None] * state_in + local_end
    return (mixed.reshape(mixed.shape[0], DI), state_end)


def body(
    inputs,
    norm_gain,
    z_weight,
    xbc_weight,
    dt_weight,
    conv_weight,
    conv_bias,
    dt_bias,
    a_log,
    skip_gain,
    gate_gain,
    out_weight,
    segments,
    cotangent,
):
    seqs_here, span_len, width = inputs.shape
    rows = seqs_here * span_len
    flat = inputs.astype(jnp.float32).reshape(rows, width)
    normed = input_norm(flat, norm_gain).astype(jnp.bfloat16)
    mesh_shape = (lax.axis_size("seq"), lax.axis_size("span"))
    dt_wide = up_to(H, 128)
    zdt_all, xbc_all, out_all = gather_rows(
        (
            jnp.concatenate([z_weight, pad_columns(dt_weight, dt_wide)], axis=1),
            xbc_weight,
            out_weight,
        ),
        mesh_shape,
    )
    zdt_all = zdt_all.reshape(-1, DI + dt_wide)
    xbc_all = xbc_all.reshape(-1, CH)
    out_all = out_all.reshape(-1, width)
    gate_dt = jnp.dot(normed, zdt_all, preferred_element_type=jnp.float32)
    gate, dt_raw = gate_dt[:, :DI], gate_dt[:, DI : DI + H]
    conv_wide = jnp.dot(normed, xbc_all, preferred_element_type=jnp.float32)
    conv_in = conv_wide.astype(jnp.bfloat16).reshape(seqs_here, span_len, CH)
    seg_wire = (segments[:, span_len - KW + 1 :] + 1).astype(jnp.bfloat16)
    edge, seg_edge = shifted((conv_in[:, span_len - KW + 1 :], seg_wire), "span", 1)
    conv_float = conv_in.astype(jnp.float32)
    edge_float = edge.astype(jnp.float32)
    seg_edge_float = seg_edge.astype(jnp.float32)
    seg_now = (segments + 1).astype(jnp.float32)
    dt_spans = dt_raw.reshape(seqs_here, span_len, H)
    prepare = jax.vmap(conv_and_step, in_axes=(0, 0, 0, 0, None, None, 0, None, None))
    activated, step_size, log_decay = prepare(
        conv_float,
        edge_float,
        seg_now,
        seg_edge_float,
        conv_weight,
        conv_bias,
        dt_spans,
        dt_bias,
        a_log,
    )
    local_scan = jax.vmap(scan_local, in_axes=(0, 0, 0, 0, 0, None))
    result, local_end, carried = local_scan(
        activated, step_size, log_decay, seg_now, seg_edge_float[:, -1], skip_gain
    )
    decay_total = carried[:, -1]
    state_in = carried_in(decay_total, local_end, "span", False)
    out_state = activated[:, :, DI + N :]
    mixed = jax.vmap(add_carry)(result, carried, out_state, state_in).reshape(rows, DI)
    mix_bf = gated_norm(mixed, gate, gate_gain).astype(jnp.bfloat16)
    columns = mix_bf
    projected = jnp.dot(
        columns,
        out_all,
        preferred_element_type=jnp.float32,
    )
    output = (flat + projected).astype(jnp.bfloat16).reshape(inputs.shape)
    grad_out = cotangent.reshape(rows, width)
    grad_mix = lax.dot_general(
        grad_out,
        out_all,
        CONTRACT_LAST,
        preferred_element_type=jnp.float32,
    )
    unused_norm, gate_pull = jax.vjp(gated_norm, mixed, gate, gate_gain)
    grad_mixed, grad_gate, gate_gain_grad = gate_pull(grad_mix)
    grad_heads = grad_mixed.reshape(seqs_here, span_len, H, P_SIZE)
    summary = jnp.einsum("sth,sthp,stn->shpn", carried, grad_heads, out_state, precision=HIGHEST)
    state_grad = carried_in(decay_total, summary, "span", True)

    def local_span(conv_a, edge_a, dt_a, weight_a, bias_a, dtb_a, alog_a, skip_a, state_a):
        batched = jax.vmap(span_full, in_axes=(0, 0, 0, None, None, None, None, None, 0, 0, 0))
        return batched(
            conv_a,
            edge_a,
            dt_a,
            weight_a,
            bias_a,
            dtb_a,
            alog_a,
            skip_a,
            state_a,
            seg_now,
            seg_edge_float,
        )

    unused_span, span_pull = jax.vjp(
        local_span,
        conv_float,
        edge_float,
        dt_spans,
        conv_weight,
        conv_bias,
        dt_bias,
        a_log,
        skip_gain,
        state_in,
    )
    grads = span_pull((grad_mixed.reshape(seqs_here, span_len, DI), state_grad))
    edge_back = shifted(grads[1], "span", -1)
    conv_grad = grads[0].at[:, span_len - KW + 1 :].add(edge_back)
    gate_bf = grad_gate.astype(jnp.bfloat16)
    conv_bf = conv_grad.reshape(rows, CH).astype(jnp.bfloat16)
    dt_bf = grads[2].reshape(rows, H).astype(jnp.bfloat16)
    dt_padded = pad_columns(dt_bf, dt_wide)
    normed_grad = lax.dot_general(
        jnp.concatenate([gate_bf, dt_padded], axis=1),
        zdt_all,
        CONTRACT_LAST,
        preferred_element_type=jnp.float32,
    ) + lax.dot_general(conv_bf, xbc_all, CONTRACT_LAST, preferred_element_type=jnp.float32)
    unused_input, norm_pull = jax.vjp(input_norm, flat, norm_gain)
    grad_flat, norm_gain_part = norm_pull(normed_grad)
    input_grad = (grad_out.astype(jnp.float32) + grad_flat).reshape(inputs.shape)
    smalls = (norm_gain_part, grads[3], grads[4], grads[5], grads[6], grads[7], gate_gain_grad)
    zdt_grad = jnp.concatenate([gate_bf, pad_columns(dt_bf, 2 * dt_wide)], axis=1)
    pairs = ((normed, zdt_grad), (normed, conv_bf), (mix_bf, grad_out))
    widths = (((0, DI), (DI, H)), ((0, CH),), ((0, width),))
    devices = mesh_shape[0] * mesh_shape[1]
    if scatter_room(pairs) < VMEM_ROOM and all(
        left.shape[1] // devices % 8 == 0 and left.shape[1] % 256 == 0 for left, right in pairs
    ):
        results = scatter_sums(
            pairs, widths, [a.reshape(-1, a.shape[-1]) for a in smalls], mesh_shape
        )
        z_weight_grad, dt_weight_grad, xbc_weight_grad, out_weight_grad = results[:4]
        summed = [r.reshape(a.shape) for r, a in zip(results[4:], smalls)]
    else:
        zdt_own, xbc_weight_grad, out_weight_grad = tuple(
            lax.psum_scatter(
                lax.dot_general(left, right, CONTRACT_FIRST, preferred_element_type=jnp.float32),
                AXES,
                scatter_dimension=0,
                tiled=True,
            )
            for left, right in pairs
        )
        z_weight_grad, dt_weight_grad = zdt_own[:, :DI], zdt_own[:, DI : DI + H]
        summed = lax.psum(smalls, AXES)
    return (
        output,
        input_grad,
        summed[0],
        z_weight_grad,
        xbc_weight_grad,
        dt_weight_grad,
        summed[1],
        summed[2],
        summed[3],
        summed[4],
        summed[5],
        summed[6],
        out_weight_grad,
    )


def solution(mesh):
    in_specs = (
        P("seq", "span", None),
        P(),
        P(("seq", "span"), None),
        P(("seq", "span"), None),
        P(("seq", "span"), None),
        P(),
        P(),
        P(),
        P(),
        P(),
        P(),
        P(("seq", "span"), None),
        P("seq", "span"),
        P("seq", "span", None),
    )
    out_specs = (
        P("seq", "span", None),
        P("seq", "span", None),
        P(),
        P(("seq", "span"), None),
        P(("seq", "span"), None),
        P(("seq", "span"), None),
        P(),
        P(),
        P(),
        P(),
        P(),
        P(),
        P(("seq", "span"), None),
    )
    return jax.shard_map(body, mesh=mesh, in_specs=in_specs, out_specs=out_specs, check_vma=False)
```
